32 devices in a mesh: seq: 16 (over z, x, core), chan: 2 (over y).
Axes of the slice: x: 2, y: 2, z: 4, core: 2. Of those that a mesh axis runs over, the one named last changes fastest.
Arguments:
- hidden: bfloat16 [2, 8192, 2048], P(None, 'seq'), may hold values from -6 to 6
- nucleotides: int32 [8192], P('seq'), may hold values from 0 to 3
- base_embed: bfloat16 [4, 2048], replicated, may hold values from -6 to 6
- x_proj: bfloat16 [2048, 4096], P(None, 'chan'), may hold values from -0.125 to 0.125
- gate_proj: bfloat16 [2048, 4096], P(None, 'chan'), may hold values from -0.125 to 0.125
- bc_proj: bfloat16 [2048, 256], replicated, may hold values from -0.125 to 0.125
- conv_x: float32 [4, 4096], P(None, 'chan'), may hold values from -1.5 to 1.5
- bias_x: float32 [4096], P('chan'), may hold values from -0.35 to -0.15
- conv_bc: float32 [4, 256], replicated, may hold values from -1.5 to 1.5
- bias_bc: float32 [256], replicated, may hold values from -0.35 to -0.15
- log_decay: bfloat16 [2, 64, 8192], P(None, 'chan', 'seq'), may hold values from -1 to 0
- d_skip: float32 [64], P('chan'), may hold values from 0.1 to 0.4
- out_proj: bfloat16 [4096, 2048], P('chan'), may hold values from -0.5 to 0.5
Outputs:
- mixed: bfloat16 [2048, 8192], P('chan', 'seq')
The draws below stay inside these ranges and needn't reach their ends.
All inputs are finite; a program needn't handle non-finite values.
Results may differ from the reference program's by a relative error of at most 0.015.
Values may be sent and summed in bfloat16 or wider, within the bound.
A program may use at most 192 MiB of HBM per device.

```python
import math
import jax
import jax.numpy as jnp
from jax import lax

D = 2048
SSM_HEAD_COUNT = 64
HEAD_DIM = 64
NS = 128
KERNEL = 4
SPAN = 256
L_DEV = 512
E = 4096
SEQUENCE_LENGTH = 8192
N_CHAN = 2


def draw_log_decay(key, part):
    random_keys = jax.random.split(key, 5)
    share_fast = 0.5
    quick_heads = jax.random.uniform(random_keys[0], (2, SSM_HEAD_COUNT, 1)) < share_fast
    baseline_rate = jnp.where(quick_heads, 1.0 / 40.0, 0.4 / SEQUENCE_LENGTH)
    blocks = SEQUENCE_LENGTH // L_DEV
    multiplier = jnp.exp(jax.random.uniform(random_keys[1], (2, SSM_HEAD_COUNT, blocks), minval=math.log(0.5), maxval=math.log(2.0)))
    multiplier = jnp.repeat(multiplier, L_DEV, axis=2)
    noise_offset = jax.random.uniform(random_keys[2], (2, SSM_HEAD_COUNT, SEQUENCE_LENGTH), minval=0.5, maxval=1.5)
    spike_locations = jax.random.randint(random_keys[3], (2, SSM_HEAD_COUNT, 2, 1), 0, SEQUENCE_LENGTH)
    spike_drops = jax.random.uniform(random_keys[4], (2, SSM_HEAD_COUNT, 2, 1), minval=math.log(0.5), maxval=math.log(0.8))
    sequence_offsets = jnp.arange(SEQUENCE_LENGTH, dtype=jnp.int32)[None, None, None, :]
    spike_events = jnp.sum(jnp.where(sequence_offsets == spike_locations, spike_drops, 0.0), axis=2)
    drawn = jnp.clip(-baseline_rate * multiplier * noise_offset + spike_events, -1.0, 0.0)
    return drawn.astype(jnp.bfloat16)


def touch_ends(values, key, least, largest):
    longest = values.shape.index(max(values.shape))
    spots = []
    for shift in (0, 1):
        where = [jax.random.randint(jax.random.fold_in(key, axis), (), 0, length) for axis, length in enumerate(values.shape)]
        where[longest] = (where[longest] + shift) % values.shape[longest]
        spots.append(tuple(where))
    return values.at[spots[0]].set(least).at[spots[1]].set(largest)


def shard_levels(key, shape, shards, smallest, high):
    level = 1.0
    for dim, shards_of in shards:
        draws = jax.random.uniform(jax.random.fold_in(jax.random.fold_in(key, 6), dim), (shards_of,), jnp.float32, smallest / len(shards), high / len(shards))
        level = level * jnp.repeat(jnp.exp(draws), shape[dim] // shards_of).reshape((-1,) + (1,) * (len(shape) - 1 - dim))
    return level


def scatter_about(stream_key, extent, deviation, bound, shards=(), held_as=jnp.bfloat16):
    result = deviation * jax.random.normal(stream_key, extent, jnp.float32)
    if shards:
        result = result * shard_levels(stream_key, extent, shards, -0.22, 0.18)
    return jnp.clip(result, -bound, bound).astype(held_as)


def setup_inputs(seed: int = 0) -> dict:
    key_of = jax.random.split(jax.random.key(seed), 14)
    return {
        "hidden": scatter_about(key_of[0], (2, SEQUENCE_LENGTH, D), 1.0, 6.0, ((1, 16),)),
        "nucleotides": touch_ends(jax.random.randint(key_of[1], (SEQUENCE_LENGTH,), 0, 4), jax.random.fold_in(key_of[1], 1), 0, 3).astype(jnp.int32),
        "base_embed": scatter_about(key_of[2], (4, D), 1.0, 6.0),
        "x_proj": scatter_about(key_of[3], (D, E), D ** -0.5, 0.125, ((1, 2),)),
        "gate_proj": scatter_about(key_of[4], (D, E), D ** -0.5, 0.125, ((1, 2),)),
        "bc_proj": scatter_about(key_of[5], (D, 2 * NS), D ** -0.5, 0.125),
        "conv_x": scatter_about(key_of[6], (KERNEL, E), 0.25, 1.5, ((1, 2),), jnp.float32),
        "bias_x": jnp.clip(-0.35 + 0.19999999 * jax.random.uniform(key_of[7], (E,), jnp.float32) ** shard_levels(key_of[7], (E,), ((0, 2),), -0.2, 0.2), -0.35, -0.15),
        "conv_bc": scatter_about(key_of[8], (KERNEL, 2 * NS), 0.25, 1.5, (), jnp.float32),
        "bias_bc": jnp.clip(jax.random.uniform(key_of[9], (2 * NS,), jnp.float32, -0.35, -0.15), -0.35, -0.15),
        "log_decay": draw_log_decay(jax.random.fold_in(key_of[13], 71), 0),
        "d_skip": jnp.clip(0.1 + 0.3 * jax.random.uniform(key_of[11], (SSM_HEAD_COUNT,), jnp.float32) ** shard_levels(key_of[11], (SSM_HEAD_COUNT,), ((0, 2),), -0.2, 0.2), 0.1, 0.4),
        "out_proj": scatter_about(key_of[12], (E, D), (E // 32) ** -0.5, 0.5, ((0, 2),)),
    }


def strand_inputs(hidden_rows, id_rows, base_embed):
    id_codes = jnp.arange(4, dtype=jnp.int32)
    onehot = (id_rows[:, None] == id_codes[None, :]).astype(jnp.bfloat16)
    looked = jnp.dot(onehot, base_embed, preferred_element_type=jnp.float32)
    return (hidden_rows.astype(jnp.float32) + looked).astype(jnp.bfloat16)

def convolve(extended, conv_weight, conv_bias, length):
    conv_sum = conv_bias.astype(jnp.float32)
    for tap_index in range(conv_weight.shape[0]):
        conv_sum = conv_sum + conv_weight[tap_index] * extended[:, tap_index:tap_index + length].astype(jnp.float32)
    return jax.nn.silu(conv_sum).astype(jnp.bfloat16)

def block_scan(x_conv, b_rows, c_rows, rate_rows):
    strands, length, row_width = x_conv.shape
    head_count = rate_rows.shape[1]
    head_width = row_width // head_count
    state_width = b_rows.shape[-1]
    block_count = length // SPAN
    inv_root = state_width ** (-0.5)
    x_blocks = x_conv.reshape(strands, block_count, SPAN, head_count, head_width).transpose(1, 0, 2, 3, 4)
    b_blocks = b_rows.reshape(strands, block_count, SPAN, state_width).transpose(1, 0, 2, 3)
    c_blocks = c_rows.reshape(strands, block_count, SPAN, state_width).transpose(1, 0, 2, 3)
    g_blocks = rate_rows.reshape(strands, head_count, block_count, SPAN).transpose(2, 0, 1, 3)
    row_ids = lax.broadcasted_iota(jnp.int32, (SPAN, SPAN), 0)
    col_ids = lax.broadcasted_iota(jnp.int32, (SPAN, SPAN), 1)
    lower_mask = row_ids >= col_ids
    highest = lax.Precision.HIGHEST

    def block_step(carry_state, blk_args):
        x_blk, b_blk, c_blk, g_blk = blk_args
        cum_log = jnp.cumsum(g_blk, axis=-1)
        inject = jnp.sqrt(-jnp.expm1(2.0 * g_blk))
        scores = jnp.einsum('sqn,skn->sqk', c_blk.astype(jnp.float32), b_blk.astype(jnp.float32), precision=highest)
        log_gap = cum_log[..., :, None] - cum_log[..., None, :]
        decay_mask = jnp.where(lower_mask, jnp.exp(jnp.where(lower_mask, log_gap, 0.0)), 0.0)
        weights = (scores[:, None] * decay_mask * (inject * inv_root)[:, :, None, :]).astype(jnp.bfloat16)
        intra_term = jnp.einsum('shqk,skhp->sqhp', weights.astype(jnp.float32), x_blk.astype(jnp.float32), precision=highest)
        carried = jnp.einsum('sqn,shpn->sqhp', c_blk.astype(jnp.float32), carry_state, precision=highest)
        carried = carried * (jnp.exp(cum_log) * inv_root).transpose(0, 2, 1)[..., None]
        tail_scale = jnp.exp(cum_log[..., -1:] - cum_log) * inject
        scaled = x_blk.astype(jnp.float32) * tail_scale.transpose(0, 2, 1)[..., None]
        fresh_state = jnp.einsum('skhp,skn->shpn', scaled, b_blk.astype(jnp.float32), precision=highest)
        carry_state = jnp.exp(cum_log[..., -1])[..., None, None] * carry_state + fresh_state
        return (carry_state, intra_term + carried)
    zero_state = jnp.zeros((strands, head_count, head_width, state_width), jnp.float32)
    final_state, y_local = lax.scan(block_step, zero_state, (x_blocks, b_blocks, c_blocks, g_blocks))
    y_local = y_local.transpose(1, 0, 2, 3, 4).reshape(strands, length, head_count, head_width)
    return (y_local, final_state)

def reference(hidden, nucleotides, base_embed, x_proj, gate_proj, bc_proj, conv_x, bias_x, conv_bc, bias_bc, log_decay, d_skip, out_proj):
    strand_zero = strand_inputs(hidden[0], nucleotides, base_embed)
    strand_one = strand_inputs(hidden[1], 3 - nucleotides, base_embed)[::-1]
    inputs = jnp.stack([strand_zero, strand_one])
    rate_rows = jnp.stack([log_decay[0], log_decay[1][:, ::-1]]).astype(jnp.float32)
    flat_rows = inputs.reshape(2 * SEQUENCE_LENGTH, D)
    x_pre = jnp.dot(flat_rows, x_proj, preferred_element_type=jnp.float32).astype(jnp.bfloat16).reshape(2, SEQUENCE_LENGTH, E)
    z_pre = jnp.dot(flat_rows, gate_proj, preferred_element_type=jnp.float32).astype(jnp.bfloat16).reshape(2, SEQUENCE_LENGTH, E)
    bc_pre = jnp.dot(flat_rows, bc_proj, preferred_element_type=jnp.float32).astype(jnp.bfloat16).reshape(2, SEQUENCE_LENGTH, 2 * NS)
    kernel = conv_x.shape[0]
    x_ext = jnp.concatenate([jnp.zeros((2, kernel - 1, E), jnp.bfloat16), x_pre], axis=1)
    bc_ext = jnp.concatenate([jnp.zeros((2, kernel - 1, 2 * NS), jnp.bfloat16), bc_pre], axis=1)
    x_conv = convolve(x_ext, conv_x, bias_x, SEQUENCE_LENGTH)
    bc_conv = convolve(bc_ext, conv_bc, bias_bc, SEQUENCE_LENGTH)
    y_local, final_state = block_scan(x_conv, bc_conv[..., :NS], bc_conv[..., NS:], rate_rows)
    ssm = y_local + d_skip[None, None, :, None] * x_conv.reshape(2, SEQUENCE_LENGTH, SSM_HEAD_COUNT, HEAD_DIM).astype(jnp.float32)
    gated = (ssm.reshape(2, SEQUENCE_LENGTH, E) * jax.nn.silu(z_pre.astype(jnp.float32))).astype(jnp.bfloat16)
    forward_out = gated[0]
    reverse_out = gated[1][::-1]
    group_width = E // N_CHAN
    contract_dims = (((0,), (1,)), ((), ()))
    total_sum = jnp.zeros((D, SEQUENCE_LENGTH), jnp.float32)
    for group_index in range(N_CHAN):
        low = group_index * group_width
        w_rows = out_proj[low:low + group_width]
        part_sum = lax.dot_general(w_rows, forward_out[:, low:low + group_width], contract_dims, preferred_element_type=jnp.float32)
        part_sum = part_sum + lax.dot_general(w_rows, reverse_out[:, low:low + group_width], contract_dims, preferred_element_type=jnp.float32)
        part_sum = lax.optimization_barrier(part_sum.astype(jnp.bfloat16))
        total_sum = total_sum + part_sum.astype(jnp.float32)
    return total_sum.astype(jnp.bfloat16)
```

```python
import functools

import jax
import jax.numpy as jnp
from jax import lax
from jax.experimental import pallas as pl
from jax.experimental.pallas import tpu as pltpu
from jax.sharding import PartitionSpec as P

CHUNK = 128
WIDTH = 256
LOG2E = 1.4426950408889634


def silu(v):
    return v * (0.5 + 0.5 * jnp.tanh(0.5 * v))


def strand_inputs(hidden_rows, ids, base_embed):
    table = base_embed.astype(jnp.float32)
    pick = ids[:, None]
    low = jnp.where(pick == 0, table[0], table[1])
    high = jnp.where(pick == 2, table[2], table[3])
    looked = jnp.where(pick < 2, low, high)
    return (hidden_rows.astype(jnp.float32) + looked).astype(jnp.bfloat16)


def spread(cols, first, heads, head_dim):
    rows = cols.shape[0]
    per = 128 // head_dim
    lane = lax.broadcasted_iota(jnp.int32, (rows, 128), 1)
    tiles = []
    for t in range(heads // per):
        tile = jnp.broadcast_to(cols[:, first + t * per : first + t * per + 1], (rows, 128))
        for p in range(1, per):
            h = first + t * per + p
            tile = jnp.where(
                lane >= p * head_dim, jnp.broadcast_to(cols[:, h : h + 1], (rows, 128)), tile
            )
        tiles.append(tile)
    return jnp.concatenate(tiles, axis=1)


def state_kernel(head_dim, x_ref, rim_ref, taps_ref, bias_ref, tail_ref, bt_ref, conv_ref, state_ref, ext):
    strands, length, width = x_ref.shape
    taps = taps_ref.shape[0]
    heads = width // head_dim
    for s in range(strands):
        ext[8 : 8 + length] = x_ref[s].astype(jnp.float32)
        if s == 0:
            ext[0:8] = rim_ref[s].astype(jnp.float32)
        else:
            ext[8 + length : 16 + length] = rim_ref[s].astype(jnp.float32)
        for c in range(length // CHUNK):
            total = jnp.broadcast_to(bias_ref[...], (CHUNK, width))
            for k in range(taps):
                shift = k - (taps - 1) if s == 0 else (taps - 1) - k
                start = 8 + c * CHUNK + shift
                total = total + taps_ref[k : k + 1] * ext[start : start + CHUNK]
            rows = slice(c * CHUNK, (c + 1) * CHUNK)
            x = silu(total).astype(jnp.bfloat16)
            conv_ref[s, rows] = x
            scale = spread(tail_ref[0, rows], s * heads, heads, head_dim)
            xs = (x.astype(jnp.float32) * scale).astype(jnp.bfloat16)
            part = jnp.dot(bt_ref[s, :, rows], xs, preferred_element_type=jnp.float32)
            if c == 0:
                acc = part
            else:
                acc = acc + part
        state_ref[s] = acc.astype(state_ref.dtype)


def scan_kernel(head_dim, x_ref, z_ref, cols_ref, rows_ref, bt_ref, c_ref, in_ref, chunk_ref, skip_ref, out_ref, scores, held):
    strands, length, width = x_ref.shape
    heads = width // head_dim
    per = 128 // head_dim
    chunks = length // CHUNK

    @pl.when(pl.program_id(0) == 0)
    def _():
        t = lax.broadcasted_iota(jnp.int32, (CHUNK, CHUNK), 0)
        r = lax.broadcasted_iota(jnp.int32, (CHUNK, CHUNK), 1)
        for s in range(strands):
            keep = (r <= t) if s == 0 else (r >= t)
            for c in range(chunks):
                rows = slice(c * CHUNK, (c + 1) * CHUNK)
                sc = jnp.dot(c_ref[s, rows], bt_ref[s, :, rows], preferred_element_type=jnp.float32)
                scores[s, c] = jnp.where(keep, sc, 0.0)

    lane = lax.broadcasted_iota(jnp.int32, (CHUNK, 128), 1)
    for s in range(strands):
        state = in_ref[s]
        order = range(chunks) if s == 0 else range(chunks - 1, -1, -1)
        for step, c in enumerate(order):
            rows = slice(c * CHUNK, (c + 1) * CHUNK)
            cols = cols_ref[0, rows]
            base = s * 3 * heads
            x = x_ref[s, rows]
            sc = scores[s, c]
            carried = jnp.dot(
                c_ref[s, rows], state.astype(jnp.bfloat16), preferred_element_type=jnp.float32
            )
            y = carried * spread(cols, base + heads, heads, head_dim)
            y = y + skip_ref[...] * x.astype(jnp.float32)
            tiles = []
            for t in range(heads // per):
                xt = x[:, t * 128 : (t + 1) * 128]
                lhs, rhs = [], []
                for p in range(per):
                    h = t * per + p
                    gap = cols[:, base + h : base + h + 1] + rows_ref[0, s * heads + h : s * heads + h + 1, rows]
                    lhs.append((sc * jnp.exp2(jnp.minimum(gap, 0.0))).astype(jnp.bfloat16))
                    inside = (lane >= p * head_dim) & (lane < (p + 1) * head_dim)
                    rhs.append(jnp.where(inside, xt, jnp.zeros_like(xt)))
                tiles.append(
                    jnp.dot(
                        jnp.concatenate(lhs, axis=1),
                        jnp.concatenate(rhs, axis=0),
                        preferred_element_type=jnp.float32,
                    )
                )
            y = y + jnp.concatenate(tiles, axis=1)
            gated = y * silu(z_ref[s, rows].astype(jnp.float32))
            if s == 0:
                held[rows] = gated
            else:
                out_ref[rows] = (held[rows] + gated).astype(out_ref.dtype)
            if step < chunks - 1:
                scale = spread(cols, base + 2 * heads, heads, head_dim)
                xs = (x.astype(jnp.float32) * scale).astype(jnp.bfloat16)
                fresh = jnp.dot(bt_ref[s, :, rows], xs, preferred_element_type=jnp.float32)
                at = s * chunks + c
                state = chunk_ref[at : at + 1] * state + fresh


def neighbours(low_rows, high_rows):
    count = lax.axis_size("seq")
    forward = [(i, i + 1) for i in range(count - 1)]
    backward = [(i + 1, i) for i in range(count - 1)]
    return lax.ppermute(low_rows, "seq", forward), lax.ppermute(high_rows, "seq", backward)


def per_device(
    hidden, nucleotides, base_embed, x_proj, gate_proj, bc_proj, conv_x, bias_x, conv_bc,
    bias_bc, log_decay, d_skip, out_proj,
):
    taps, inner = conv_x.shape
    length = hidden.shape[1]
    head_count = d_skip.shape[0]
    head_dim = inner // head_count
    states = conv_bc.shape[1] // 2
    width = min(WIDTH, inner)
    blocks = inner // width
    heads = width // head_dim
    chunks = length // CHUNK
    inv_root = states ** (-0.5)
    count = lax.axis_size("seq")
    me = lax.axis_index("seq")

    r = jnp.arange(length)
    rates = log_decay.astype(jnp.float32)
    same = (r[:, None] // CHUNK) == (r[None, :] // CHUNK)
    older = [r[:, None] <= r[None, :], r[:, None] >= r[None, :]]

    def sums(masks):
        return jnp.stack(
            [
                jnp.dot(log_decay[s], masks[s].astype(jnp.bfloat16), preferred_element_type=jnp.float32)
                for s in range(2)
            ]
        )

    cum = sums([same & older[0], same & older[1]])
    left = sums([same & (r[:, None] > r[None, :]), same & (r[:, None] < r[None, :])])
    left_all = sums([r[:, None] > r[None, :], r[:, None] < r[None, :]])
    inject = jnp.sqrt(-jnp.expm1(2.0 * rates))
    totals = jnp.sum(rates, axis=2)
    gathered_totals = lax.all_gather(totals, "seq")
    tail_all = jnp.exp(left_all) * inject
    tail = jnp.exp(left) * inject
    entry = jnp.exp(cum) * inv_root
    row_terms = jnp.log2(inject * inv_root) - cum * LOG2E
    rows_arr = row_terms.reshape(2, blocks, heads, length).transpose(1, 0, 2, 3)
    rows_arr = rows_arr.reshape(blocks, 2 * heads, length)
    cols_arr = jnp.stack([cum * LOG2E, entry, tail], axis=1)
    cols_arr = cols_arr.reshape(2, 3, blocks, heads, length).transpose(2, 4, 0, 1, 3)
    cols_arr = cols_arr.reshape(blocks, length, 6 * heads)
    tail_arr = tail_all.reshape(2, blocks, heads, length).transpose(1, 3, 0, 2)
    tail_arr = tail_arr.reshape(blocks, length, 2 * heads)
    chunk_decay = jnp.exp(jnp.sum(rates.reshape(2, head_count, chunks, CHUNK), axis=3))
    chunk_decay = jnp.repeat(chunk_decay.transpose(0, 2, 1).reshape(2 * chunks, head_count), head_dim, axis=1)
    skip = jnp.repeat(d_skip, head_dim)[None]

    inputs = jnp.concatenate(
        [
            strand_inputs(hidden[0], nucleotides, base_embed),
            strand_inputs(hidden[1], 3 - nucleotides, base_embed),
        ],
        axis=0,
    )
    inputs = lax.optimization_barrier(inputs)

    def project(weight):
        out = jnp.dot(inputs, weight, preferred_element_type=jnp.float32)
        return out.astype(jnp.bfloat16).reshape(2, length, -1)

    bc_pre = project(bc_proj)
    x_pre = project(x_proj)
    edge = taps - 1
    low = jnp.concatenate([x_pre[0, -edge:], bc_pre[0, -edge:]], axis=1)
    high = jnp.concatenate([x_pre[1, :edge], bc_pre[1, :edge]], axis=1)
    low, high = neighbours(low, high)
    x_rim = jnp.stack(
        [
            jnp.pad(low[:, :inner], ((8 - edge, 0), (0, 0))),
            jnp.pad(high[:, :inner], ((0, 8 - edge), (0, 0))),
        ]
    )
    bc_ext = [
        jnp.concatenate([low[:, inner:], bc_pre[0]], axis=0),
        jnp.concatenate([bc_pre[1], high[:, inner:]], axis=0),
    ]
    bc_conv = []
    for s in range(2):
        total = bias_bc
        for k in range(taps):
            at = k if s == 0 else edge - k
            total = total + conv_bc[k] * bc_ext[s][at : at + length].astype(jnp.float32)
        bc_conv.append(jax.nn.silu(total).astype(jnp.bfloat16))
    bc_conv = jnp.stack(bc_conv)
    c_rows = bc_conv[..., states:]
    b_cols = bc_conv[..., :states].transpose(0, 2, 1)

    params = pltpu.CompilerParams(dimension_semantics=("arbitrary",), vmem_limit_bytes=48 * 1024 * 1024)
    wide = pl.BlockSpec((2, length, width), lambda i: (0, 0, i))
    whole = lambda a: pl.BlockSpec(a.shape, lambda i: (0,) * a.ndim)
    x_conv, local = pl.pallas_call(
        functools.partial(state_kernel, head_dim),
        grid=(blocks,),
        out_shape=(
            jax.ShapeDtypeStruct((2, length, inner), jnp.bfloat16),
            jax.ShapeDtypeStruct((2, states, inner), jnp.bfloat16),
        ),
        in_specs=[
            wide,
            pl.BlockSpec((2, 8, width), lambda i: (0, 0, i)),
            pl.BlockSpec((taps, width), lambda i: (0, i)),
            pl.BlockSpec((1, width), lambda i: (0, i)),
            pl.BlockSpec((1, length, 2 * heads), lambda i: (i, 0, 0)),
            whole(b_cols),
        ],
        out_specs=(wide, pl.BlockSpec((2, states, width), lambda i: (0, 0, i))),
        scratch_shapes=[pltpu.VMEM((length + 16, width), jnp.float32)],
        compiler_params=params,
        name="conv_state",
    )(x_pre, x_rim, conv_x, bias_x[None], tail_arr, b_cols)

    gathered = lax.all_gather(local, "seq")
    z_pre = project(gate_proj)
    j = jnp.arange(count)
    between = jnp.stack(
        [
            (j[:, None] < j[None, :]) & (j[None, :] < me),
            (j[:, None] > j[None, :]) & (j[None, :] > me),
        ],
        axis=1,
    )
    logs = jnp.sum(
        jnp.where(between[..., None], gathered_totals.transpose(1, 0, 2)[None], 0.0), axis=2
    )
    ahead = jnp.stack([j < me, j > me], axis=1)
    factor = jnp.where(ahead[..., None], jnp.exp(logs), 0.0)
    factor = jnp.repeat(factor, head_dim, axis=2)
    incoming = jnp.sum(factor[:, :, None, :] * gathered.astype(jnp.float32), axis=0)

    mixed_in = pl.pallas_call(
        functools.partial(scan_kernel, head_dim),
        grid=(blocks,),
        out_shape=jax.ShapeDtypeStruct((length, inner), jnp.bfloat16),
        in_specs=[
            wide,
            wide,
            pl.BlockSpec((1, length, 6 * heads), lambda i: (i, 0, 0)),
            pl.BlockSpec((1, 2 * heads, length), lambda i: (i, 0, 0)),
            whole(b_cols),
            whole(c_rows),
            pl.BlockSpec((2, states, width), lambda i: (0, 0, i)),
            pl.BlockSpec((2 * chunks, width), lambda i: (0, i)),
            pl.BlockSpec((1, width), lambda i: (0, i)),
        ],
        out_specs=pl.BlockSpec((length, width), lambda i: (0, i)),
        scratch_shapes=[
            pltpu.VMEM((2, chunks, CHUNK, CHUNK), jnp.float32),
            pltpu.VMEM((length, width), jnp.float32),
        ],
        compiler_params=params,
        name="scan",
    )(x_conv, z_pre, cols_arr, rows_arr, b_cols, c_rows, incoming, chunk_decay, skip)

    def out_part(weight):
        return lax.dot_general(
            weight, mixed_in, (((0,), (1,)), ((), ())), preferred_element_type=jnp.float32
        )

    if lax.axis_size("chan") == 2:
        half = out_proj.shape[1] // 2
        mine = lax.axis_index("chan")
        theirs = out_part(lax.dynamic_slice_in_dim(out_proj, (1 - mine) * half, half, 1))
        sent = lax.ppermute(theirs.astype(jnp.bfloat16), "chan", [(0, 1), (1, 0)])
        own = out_part(lax.dynamic_slice_in_dim(out_proj, mine * half, half, 1))
        own = own.astype(jnp.bfloat16).astype(jnp.float32)
        return (own + sent.astype(jnp.float32)).astype(jnp.bfloat16)
    return lax.psum_scatter(
        out_part(out_proj).astype(jnp.bfloat16), "chan", scatter_dimension=0, tiled=True
    )


def solution(mesh):
    in_specs = (
        P(None, "seq", None), P("seq"), P(), P(None, "chan"), P(None, "chan"), P(),
        P(None, "chan"), P("chan"), P(), P(), P(None, "chan", "seq"), P("chan"), P("chan", None),
    )
    return jax.shard_map(
        per_device, mesh=mesh, in_specs=in_specs, out_specs=P("chan", "seq"), check_vma=False
    )
```

```python
import functools

import jax
import jax.numpy as jnp
from jax import lax
from jax.experimental import pallas as pl
from jax.experimental.pallas import tpu as pltpu
from jax.sharding import PartitionSpec as P

CHUNK = 128
WIDTH = 256
LOG2E = 1.4426950408889634


def silu(v):
    return v * (0.5 + 0.5 * jnp.tanh(0.5 * v))


def strand_inputs(hidden_rows, ids, base_embed):
    table = base_embed.astype(jnp.float32)
    pick = ids[:, None]
    low = jnp.where(pick == 0, table[0], table[1])
    high = jnp.where(pick == 2, table[2], table[3])
    looked = jnp.where(pick < 2, low, high)
    return (hidden_rows.astype(jnp.float32) + looked).astype(jnp.bfloat16)


def spread(cols, first, heads, head_dim):
    rows = cols.shape[0]
    per = 128 // head_dim
    lane = lax.broadcasted_iota(jnp.int32, (rows, 128), 1)
    tiles = []
    for t in range(heads // per):
        tile = jnp.broadcast_to(cols[:, first + t * per : first + t * per + 1], (rows, 128))
        for p in range(1, per):
            h = first + t * per + p
            tile = jnp.where(
                lane >= p * head_dim, jnp.broadcast_to(cols[:, h : h + 1], (rows, 128)), tile
            )
        tiles.append(tile)
    return jnp.concatenate(tiles, axis=1)


def state_kernel(head_dim, x_ref, rim_ref, taps_ref, bias_ref, tail_ref, half_ref, bt_ref, conv_ref, state_ref, mid_ref, ext):
    strands, length, width = x_ref.shape
    taps = taps_ref.shape[0]
    heads = width // head_dim
    for s in range(strands):
        ext[8 : 8 + length] = x_ref[s].astype(jnp.float32)
        if s == 0:
            ext[0:8] = rim_ref[s].astype(jnp.float32)
        else:
            ext[8 + length : 16 + length] = rim_ref[s].astype(jnp.float32)
        chunks = length // CHUNK
        for step in range(chunks):
            c = step if s == 0 else chunks - 1 - step
            total = jnp.broadcast_to(bias_ref[...], (CHUNK, width))
            for k in range(taps):
                shift = k - (taps - 1) if s == 0 else (taps - 1) - k
                start = 8 + c * CHUNK + shift
                total = total + taps_ref[k : k + 1] * ext[start : start + CHUNK]
            rows = slice(c * CHUNK, (c + 1) * CHUNK)
            x = silu(total).astype(jnp.bfloat16)
            conv_ref[s, rows] = x
            scale = spread(tail_ref[0, rows], s * heads, heads, head_dim)
            xs = (x.astype(jnp.float32) * scale).astype(jnp.bfloat16)
            part = jnp.dot(bt_ref[s, :, rows], xs, preferred_element_type=jnp.float32)
            if step == 0:
                acc = part
            else:
                acc = acc + part
            if step == chunks // 2 - 1:
                mid_ref[s] = acc
                acc = acc * half_ref[s : s + 1]
        state_ref[s] = acc.astype(state_ref.dtype)


def scan_kernel(head_dim, x_ref, z_ref, cols_ref, rows_ref, bt_ref, c_ref, in_ref, chunk_ref, skip_ref, out_ref, scores, held):
    strands, length, width = x_ref.shape
    heads = width // head_dim
    per = 128 // head_dim
    chunks = length // CHUNK

    @pl.when(pl.program_id(0) == 0)
    def _():
        t = lax.broadcasted_iota(jnp.int32, (CHUNK, CHUNK), 0)
        r = lax.broadcasted_iota(jnp.int32, (CHUNK, CHUNK), 1)
        for s in range(strands):
            keep = (r <= t) if s == 0 else (r >= t)
            for c in range(chunks):
                rows = slice(c * CHUNK, (c + 1) * CHUNK)
                sc = jnp.dot(c_ref[s, rows], bt_ref[s, :, rows], preferred_element_type=jnp.float32)
                scores[s, c] = jnp.where(keep, sc, 0.0)

    lane = lax.broadcasted_iota(jnp.int32, (CHUNK, 128), 1)
    for s in range(strands):
        state = in_ref[s]
        order = range(chunks) if s == 0 else range(chunks - 1, -1, -1)
        for step, c in enumerate(order):
            rows = slice(c * CHUNK, (c + 1) * CHUNK)
            cols = cols_ref[0, rows]
            base = s * 3 * heads
            x = x_ref[s, rows]
            sc = scores[s, c]
            carried = jnp.dot(
                c_ref[s, rows], state.astype(jnp.bfloat16), preferred_element_type=jnp.float32
            )
            y = carried * spread(cols, base + heads, heads, head_dim)
            y = y + skip_ref[...] * x.astype(jnp.float32)
            tiles = []
            for t in range(heads // per):
                xt = x[:, t * 128 : (t + 1) * 128]
                lhs, rhs = [], []
                for p in range(per):
                    h = t * per + p
                    gap = cols[:, base + h : base + h + 1] + rows_ref[0, s * heads + h : s * heads + h + 1, rows]
                    lhs.append((sc * jnp.exp2(jnp.minimum(gap, 0.0))).astype(jnp.bfloat16))
                    inside = (lane >= p * head_dim) & (lane < (p + 1) * head_dim)
                    rhs.append(jnp.where(inside, xt, jnp.zeros_like(xt)))
                tiles.append(
                    jnp.dot(
                        jnp.concatenate(lhs, axis=1),
                        jnp.concatenate(rhs, axis=0),
                        preferred_element_type=jnp.float32,
                    )
                )
            y = y + jnp.concatenate(tiles, axis=1)
            gated = y * silu(z_ref[s, rows].astype(jnp.float32))
            if s == 0:
                held[rows] = gated
            else:
                out_ref[rows] = (held[rows] + gated).astype(out_ref.dtype)
            if step < chunks - 1:
                scale = spread(cols, base + 2 * heads, heads, head_dim)
                xs = (x.astype(jnp.float32) * scale).astype(jnp.bfloat16)
                fresh = jnp.dot(bt_ref[s, :, rows], xs, preferred_element_type=jnp.float32)
                at = s * chunks + c
                state = chunk_ref[0, at : at + 1] * state + fresh


def neighbours(low_rows, high_rows):
    count = lax.axis_size("seq")
    forward = [(i, i + 1) for i in range(count - 1)]
    backward = [(i + 1, i) for i in range(count - 1)]
    return lax.ppermute(low_rows, "seq", forward), lax.ppermute(high_rows, "seq", backward)


def late_in(state, decay, fresh):
    return decay[..., None, :] * state.astype(jnp.float32) + fresh.astype(jnp.float32)


def entering(local, every):
    count = lax.axis_size("seq")
    me = lax.axis_index("seq")
    inner = local.shape[2]
    log = every
    lines = count // 4
    half = inner // 2
    core, across, line = me % 2, (me // 2) % 2, me // 4
    pair_log = jnp.sum(log.reshape(count // 2, 2, 2, inner), axis=1)
    line_log = jnp.sum(log.reshape(lines, 4, 2, inner), axis=1)

    def joined(first, second, first_log, second_log, second_is_earlier):
        flag = second_is_earlier[:, None]
        a = jnp.where(flag, 1.0, jnp.exp(second_log))[:, None, :]
        b = jnp.where(flag, jnp.exp(first_log), 1.0)[:, None, :]
        return a * first.astype(jnp.float32) + b * second.astype(jnp.float32)

    def row(table, at):
        return lax.dynamic_index_in_dim(table, at, 0, False)

    def mine(a):
        return lax.dynamic_slice_in_dim(a, core * half, half, a.ndim - 1)

    swap = [(i, i ^ 1) for i in range(count)]
    swap_pair = [(i, i ^ 2) for i in range(count)]
    up = [(i, i + 4) for i in range(count - 4)]
    down = [(i + 4, i) for i in range(count - 4)]

    other = lax.ppermute(local, "seq", swap)
    core_earlier = jnp.stack([core == 1, core == 0])
    chip = joined(
        mine(local), mine(other), mine(row(log, me)), mine(row(log, me ^ 1)), core_earlier
    ).astype(jnp.bfloat16)
    chip_other = lax.ppermute(chip, "seq", swap_pair)
    pair_me = me // 2
    pair_earlier = jnp.stack([across == 1, across == 0])
    group = joined(
        chip, chip_other, mine(row(pair_log, pair_me)), mine(row(pair_log, pair_me ^ 1)), pair_earlier
    ).astype(jnp.bfloat16)

    logs_half = mine(line_log)
    at = jnp.arange(lines)
    total = [0.0, 0.0]
    moving = [group[0], group[1]]
    for step in range(1, lines):
        moving = [lax.ppermute(moving[0], "seq", up), lax.ppermute(moving[1], "seq", down)]
        for s in range(2):
            if s == 0:
                between = (at > line - step) & (at < line)
            else:
                between = (at < line + step) & (at > line)
            factor = jnp.exp(jnp.sum(jnp.where(between[:, None], logs_half[:, s], 0.0), axis=0))
            total[s] = total[s] + factor[None, :] * moving[s].astype(jnp.float32)
    total = jnp.stack([jnp.broadcast_to(jnp.asarray(t, jnp.float32), group.shape[1:]) for t in total])
    pair_decay = mine(jnp.exp(row(pair_log, pair_me ^ 1)))
    chip_in = jnp.where(pair_earlier[:, None, None], late_in(total, pair_decay, chip_other), total)
    chip_in = chip_in.astype(jnp.bfloat16)
    rest = lax.ppermute(chip_in, "seq", swap)
    low = jnp.where(core == 0, chip_in, rest)
    high = jnp.where(core == 0, rest, chip_in)
    full = jnp.concatenate([low, high], axis=2).astype(jnp.float32)
    return jnp.where(
        core_earlier[:, None, None], late_in(full, jnp.exp(row(log, me ^ 1)), other), full
    )


def per_device(
    hidden, nucleotides, base_embed, x_proj, gate_proj, bc_proj, conv_x, bias_x, conv_bc,
    bias_bc, log_decay, d_skip, out_proj,
):
    taps, inner = conv_x.shape
    length = hidden.shape[1]
    head_count = d_skip.shape[0]
    head_dim = inner // head_count
    states = conv_bc.shape[1] // 2
    width = min(WIDTH, inner)
    blocks = inner // width
    heads = width // head_dim
    chunks = length // CHUNK
    inv_root = states ** (-0.5)

    r = jnp.arange(length)
    rates = log_decay.astype(jnp.float32)
    same = (r[:, None] // CHUNK) == (r[None, :] // CHUNK)
    older = [r[:, None] <= r[None, :], r[:, None] >= r[None, :]]

    def sums(masks):
        return jnp.stack(
            [
                jnp.dot(log_decay[s], masks[s].astype(jnp.bfloat16), preferred_element_type=jnp.float32)
                for s in range(2)
            ]
        )

    cum = sums([same & older[0], same & older[1]])
    left = sums([same & (r[:, None] > r[None, :]), same & (r[:, None] < r[None, :])])
    part = length // 2
    same_half = (r[:, None] // part) == (r[None, :] // part)
    left_half = sums([same_half & (r[:, None] > r[None, :]), same_half & (r[:, None] < r[None, :])])
    inject = jnp.sqrt(-jnp.expm1(2.0 * rates))
    totals = jnp.sum(rates, axis=2)
    every = jnp.repeat(lax.all_gather(totals, "seq"), head_dim, axis=2)
    tail_all = jnp.exp(left_half) * inject
    tail = jnp.exp(left) * inject
    entry = jnp.exp(cum) * inv_root
    row_terms = jnp.log2(inject * inv_root) - cum * LOG2E
    rows_arr = row_terms.reshape(2, blocks, heads, length).transpose(1, 0, 2, 3)
    rows_arr = rows_arr.reshape(blocks, 2 * heads, length)
    cols_arr = jnp.stack([cum * LOG2E, entry, tail], axis=1)
    cols_arr = cols_arr.reshape(2, 3, blocks, heads, length).transpose(2, 4, 0, 1, 3)
    cols_arr = cols_arr.reshape(blocks, length, 6 * heads)
    tail_arr = tail_all.reshape(2, blocks, heads, length).transpose(1, 3, 0, 2)
    tail_arr = tail_arr.reshape(blocks, length, 2 * heads)
    span_logs = jnp.sum(rates.reshape(2, head_count, chunks, CHUNK), axis=3)
    span_logs = jnp.repeat(span_logs.transpose(0, 2, 1), head_dim, axis=2)
    chunk_decay = jnp.exp(span_logs).reshape(2, 2, chunks // 2, inner).transpose(1, 0, 2, 3)
    chunk_decay = chunk_decay.reshape(2, chunks, inner)
    half_logs = jnp.sum(span_logs.reshape(2, 2, chunks // 2, inner), axis=2)
    late_half = jnp.exp(jnp.stack([half_logs[0, 1], half_logs[1, 0]]))
    early_half = jnp.exp(jnp.stack([half_logs[0, 0], half_logs[1, 1]]))
    skip = jnp.repeat(d_skip, head_dim)[None]

    inputs = jnp.concatenate(
        [
            strand_inputs(hidden[0], nucleotides, base_embed),
            strand_inputs(hidden[1], 3 - nucleotides, base_embed),
        ],
        axis=0,
    )
    inputs, every = lax.optimization_barrier((inputs, every))

    def project(weight):
        out = jnp.dot(inputs, weight, preferred_element_type=jnp.float32)
        return out.astype(jnp.bfloat16).reshape(2, length, -1)

    bc_pre = project(bc_proj)
    x_pre = project(x_proj)
    edge = taps - 1
    low = jnp.concatenate([x_pre[0, -edge:], bc_pre[0, -edge:]], axis=1)
    high = jnp.concatenate([x_pre[1, :edge], bc_pre[1, :edge]], axis=1)
    low, high = neighbours(low, high)
    x_rim = jnp.stack(
        [
            jnp.pad(low[:, :inner], ((8 - edge, 0), (0, 0))),
            jnp.pad(high[:, :inner], ((0, 8 - edge), (0, 0))),
        ]
    )
    bc_ext = [
        jnp.concatenate([low[:, inner:], bc_pre[0]], axis=0),
        jnp.concatenate([bc_pre[1], high[:, inner:]], axis=0),
    ]
    bc_conv = []
    for s in range(2):
        total = bias_bc
        for k in range(taps):
            at = k if s == 0 else edge - k
            total = total + conv_bc[k] * bc_ext[s][at : at + length].astype(jnp.float32)
        bc_conv.append(jax.nn.silu(total).astype(jnp.bfloat16))
    bc_conv = jnp.stack(bc_conv)
    c_rows = bc_conv[..., states:]
    b_cols = bc_conv[..., :states].transpose(0, 2, 1)

    params = pltpu.CompilerParams(dimension_semantics=("arbitrary",), vmem_limit_bytes=48 * 1024 * 1024)
    wide = pl.BlockSpec((2, length, width), lambda i: (0, 0, i))
    state_block = pl.BlockSpec((2, states, width), lambda i: (0, 0, i))
    whole = lambda a: pl.BlockSpec(a.shape, lambda i: (0,) * a.ndim)
    x_conv, local, mid = pl.pallas_call(
        functools.partial(state_kernel, head_dim),
        grid=(blocks,),
        out_shape=(
            jax.ShapeDtypeStruct((2, length, inner), jnp.bfloat16),
            jax.ShapeDtypeStruct((2, states, inner), jnp.bfloat16),
            jax.ShapeDtypeStruct((2, states, inner), jnp.float32),
        ),
        in_specs=[
            wide,
            pl.BlockSpec((2, 8, width), lambda i: (0, 0, i)),
            pl.BlockSpec((taps, width), lambda i: (0, i)),
            pl.BlockSpec((1, width), lambda i: (0, i)),
            pl.BlockSpec((1, length, 2 * heads), lambda i: (i, 0, 0)),
            pl.BlockSpec((2, width), lambda i: (0, i)),
            whole(b_cols),
        ],
        out_specs=(wide, state_block, state_block),
        scratch_shapes=[pltpu.VMEM((length + 16, width), jnp.float32)],
        compiler_params=params,
        name="conv_state",
    )(x_pre, x_rim, conv_x, bias_x[None], tail_arr, late_half, b_cols)

    z_pre = project(gate_proj)
    incoming = entering(local, every)
    entry_half = [
        jnp.stack([incoming[0], late_in(incoming[1], early_half[1], mid[1])]),
        jnp.stack([late_in(incoming[0], early_half[0], mid[0]), incoming[1]]),
    ]

    def scan_half(half):
        rows_spec = pl.BlockSpec((2, part, width), lambda i: (0, half, i))
        return pl.pallas_call(
            functools.partial(scan_kernel, head_dim),
            grid=(blocks,),
            out_shape=jax.ShapeDtypeStruct((part, inner), jnp.bfloat16),
            in_specs=[
                rows_spec,
                rows_spec,
                pl.BlockSpec((1, part, 6 * heads), lambda i: (i, half, 0)),
                pl.BlockSpec((1, 2 * heads, part), lambda i: (i, 0, half)),
                pl.BlockSpec((2, states, part), lambda i: (0, 0, half)),
                pl.BlockSpec((2, part, states), lambda i: (0, half, 0)),
                state_block,
                pl.BlockSpec((1, chunks, width), lambda i: (half, 0, i)),
                pl.BlockSpec((1, width), lambda i: (0, i)),
            ],
            out_specs=pl.BlockSpec((part, width), lambda i: (0, i)),
            scratch_shapes=[
                pltpu.VMEM((2, part // CHUNK, CHUNK, CHUNK), jnp.float32),
                pltpu.VMEM((part, width), jnp.float32),
            ],
            compiler_params=params,
            cost_estimate=pl.CostEstimate(
                flops=12 * part * inner * states, bytes_accessed=12 * part * inner, transcendentals=0
            ),
            name="scan",
        )(x_conv, z_pre, cols_arr, rows_arr, b_cols, c_rows, entry_half[half], chunk_decay, skip)

    def out_part(weight, rows):
        return lax.dot_general(
            weight, rows, (((0,), (1,)), ((), ())), preferred_element_type=jnp.float32
        ).astype(jnp.bfloat16)

    if lax.axis_size("chan") == 2:
        size = out_proj.shape[1] // 2
        mine = lax.axis_index("chan")
        send_weight = lax.dynamic_slice_in_dim(out_proj, (1 - mine) * size, size, 1)
        own_weight = lax.dynamic_slice_in_dim(out_proj, mine * size, size, 1)
        first = scan_half(0)
        sent_first = lax.ppermute(out_part(send_weight, first), "chan", [(0, 1), (1, 0)])
        second = scan_half(1)
        sent_second = lax.ppermute(out_part(send_weight, second), "chan", [(0, 1), (1, 0)])
        own = lax.optimization_barrier(out_part(own_weight, jnp.concatenate([first, second])))
        sent = jnp.concatenate([sent_first, sent_second], axis=1)
        return (own.astype(jnp.float32) + sent.astype(jnp.float32)).astype(jnp.bfloat16)
    mixed_in = jnp.concatenate([scan_half(0), scan_half(1)])
    return lax.psum_scatter(
        out_part(out_proj, mixed_in), "chan", scatter_dimension=0, tiled=True
    )


def solution(mesh):
    in_specs = (
        P(None, "seq", None), P("seq"), P(), P(None, "chan"), P(None, "chan"), P(),
        P(None, "chan"), P("chan"), P(), P(), P(None, "chan", "seq"), P("chan"), P("chan", None),
    )
    return jax.shard_map(
        per_device, mesh=mesh, in_specs=in_specs, out_specs=P("chan", "seq"), check_vma=False
    )
```

```python
import functools

import jax
import jax.numpy as jnp
from jax import lax
from jax.experimental import pallas as pl
from jax.experimental.pallas import tpu as pltpu
from jax.sharding import PartitionSpec as P

CHUNK = 128
WIDTH = 256
PAD = 16
LOG2E = 1.4426950408889634


def silu(v):
    return v * (0.5 + 0.5 * jnp.tanh(0.5 * v))


def strand_inputs(hidden_rows, ids, base_embed):
    table = base_embed.astype(jnp.float32)
    pick = ids[:, None]
    low = jnp.where(pick == 0, table[0], table[1])
    high = jnp.where(pick == 2, table[2], table[3])
    looked = jnp.where(pick < 2, low, high)
    return (hidden_rows.astype(jnp.float32) + looked).astype(jnp.bfloat16)


def spread(cols, first, heads, head_dim):
    rows = cols.shape[0]
    per = 128 // head_dim
    lane = lax.broadcasted_iota(jnp.int32, (rows, 128), 1)
    tiles = []
    for t in range(heads // per):
        tile = jnp.broadcast_to(cols[:, first + t * per : first + t * per + 1], (rows, 128))
        for p in range(1, per):
            h = first + t * per + p
            tile = jnp.where(
                lane >= p * head_dim, jnp.broadcast_to(cols[:, h : h + 1], (rows, 128)), tile
            )
        tiles.append(tile)
    return jnp.concatenate(tiles, axis=1)


def state_kernel(head_dim, x_ref, rim_ref, taps_ref, bias_ref, tail_ref, decay_ref, bt_ref, conv_ref, state_ref, ext):
    strands, length, width = x_ref.shape
    taps = taps_ref.shape[0]
    heads = width // head_dim
    for s in range(strands):
        ext[8 : 8 + length] = x_ref[s].astype(jnp.float32)
        if s == 0:
            ext[0:8] = rim_ref[s].astype(jnp.float32)
        else:
            ext[8 + length : 16 + length] = rim_ref[s].astype(jnp.float32)
        chunks = length // CHUNK
        for step in range(chunks):
            c = step if s == 0 else chunks - 1 - step
            total = jnp.broadcast_to(bias_ref[...], (CHUNK, width))
            for k in range(taps):
                shift = k - (taps - 1) if s == 0 else (taps - 1) - k
                start = 8 + c * CHUNK + shift
                total = total + taps_ref[k : k + 1] * ext[start : start + CHUNK]
            rows = slice(c * CHUNK, (c + 1) * CHUNK)
            x = silu(total).astype(jnp.bfloat16)
            conv_ref[s, rows] = x
            scale = spread(tail_ref[0, rows], s * heads, heads, head_dim)
            xs = (x.astype(jnp.float32) * scale).astype(jnp.bfloat16)
            part = jnp.dot(bt_ref[s, :, rows], xs, preferred_element_type=jnp.float32)
            if step == 0:
                acc = part
            else:
                acc = acc + part
        states = acc.shape[0]
        state_ref[s, :states] = acc.astype(state_ref.dtype)
        state_ref[s, states:] = jnp.broadcast_to(
            decay_ref[s : s + 1], (PAD, width)
        ).astype(state_ref.dtype)


def scan_kernel(head_dim, s, x_ref, cols_ref, rows_ref, bt_ref, c_ref, chunk_ref, skip_ref, out_ref, scores):
    _, length, width = x_ref.shape
    heads = width // head_dim
    per = 128 // head_dim
    chunks = length // CHUNK

    @pl.when(pl.program_id(0) == 0)
    def _():
        t = lax.broadcasted_iota(jnp.int32, (CHUNK, CHUNK), 0)
        r = lax.broadcasted_iota(jnp.int32, (CHUNK, CHUNK), 1)
        keep = (r <= t) if s == 0 else (r >= t)
        for c in range(chunks):
            rows = slice(c * CHUNK, (c + 1) * CHUNK)
            sc = jnp.dot(c_ref[s, rows], bt_ref[s, :, rows], preferred_element_type=jnp.float32)
            scores[c] = jnp.where(keep, sc, 0.0)

    lane = lax.broadcasted_iota(jnp.int32, (CHUNK, 128), 1)
    state = None
    order = range(chunks) if s == 0 else range(chunks - 1, -1, -1)
    for step, c in enumerate(order):
        rows = slice(c * CHUNK, (c + 1) * CHUNK)
        cols = cols_ref[0, rows]
        base = s * 3 * heads
        x = x_ref[0, rows]
        sc = scores[c]
        y = skip_ref[...] * x.astype(jnp.float32)
        if step > 0:
            carried = jnp.dot(
                c_ref[s, rows], state.astype(jnp.bfloat16), preferred_element_type=jnp.float32
            )
            y = y + carried * spread(cols, base + heads, heads, head_dim)
        tiles = []
        for t in range(heads // per):
            xt = x[:, t * 128 : (t + 1) * 128]
            lhs, rhs = [], []
            for p in range(per):
                h = t * per + p
                gap = cols[:, base + h : base + h + 1] + rows_ref[0, s * heads + h : s * heads + h + 1, rows]
                lhs.append((sc * jnp.exp2(jnp.minimum(gap, 0.0))).astype(jnp.bfloat16))
                inside = (lane >= p * head_dim) & (lane < (p + 1) * head_dim)
                rhs.append(jnp.where(inside, xt, jnp.zeros_like(xt)))
            tiles.append(
                jnp.dot(
                    jnp.concatenate(lhs, axis=1),
                    jnp.concatenate(rhs, axis=0),
                    preferred_element_type=jnp.float32,
                )
            )
        y = y + jnp.concatenate(tiles, axis=1)
        out_ref[rows] = y.astype(out_ref.dtype)
        if step < chunks - 1:
            scale = spread(cols, base + 2 * heads, heads, head_dim)
            xs = (x.astype(jnp.float32) * scale).astype(jnp.bfloat16)
            fresh = jnp.dot(bt_ref[s, :, rows], xs, preferred_element_type=jnp.float32)
            at = s * chunks + c
            state = fresh if step == 0 else chunk_ref[at : at + 1] * state + fresh


def gate_kernel(head_dim, y_zero, y_one, z_ref, entry_ref, c_ref, in_ref, out_ref):
    strands, length, width = z_ref.shape
    y_refs = (y_zero, y_one)
    heads = width // head_dim
    for c in range(length // CHUNK):
        rows = slice(c * CHUNK, (c + 1) * CHUNK)
        total = 0.0
        for s in range(strands):
            carried = jnp.dot(c_ref[s, rows], in_ref[s], preferred_element_type=jnp.float32)
            y = y_refs[s][rows].astype(jnp.float32)
            y = y + carried * spread(entry_ref[0, rows], s * heads, heads, head_dim)
            total = total + y * silu(z_ref[s, rows].astype(jnp.float32))
        out_ref[rows] = total.astype(out_ref.dtype)


def neighbours(low_rows, high_rows):
    count = lax.axis_size("seq")
    forward = [(i, i + 1) for i in range(count - 1)]
    backward = [(i + 1, i) for i in range(count - 1)]
    return lax.ppermute(low_rows, "seq", forward), lax.ppermute(high_rows, "seq", backward)


def entering(local, states, across_work, line_work):
    count = lax.axis_size("seq")
    me = lax.axis_index("seq")
    half = local.shape[2] // 2
    core, across = me % 2, (me // 2) % 2
    row = lax.broadcasted_iota(jnp.int32, (1, local.shape[1], 1), 1)

    def decay(a):
        return a[..., states : states + 1, :].astype(jnp.float32)

    def joined(first, second, second_is_earlier):
        flag = second_is_earlier[:, None, None]
        a = jnp.where(flag, 1.0, decay(second))
        b = jnp.where(flag, decay(first), 1.0)
        first, second = first.astype(jnp.float32), second.astype(jnp.float32)
        both = jnp.where(row < states, a * first + b * second, first * second)
        return both.astype(jnp.bfloat16)

    def after(state, step, is_earlier):
        moved = decay(step) * state + step[..., :states, :].astype(jnp.float32)
        return jnp.where(is_earlier[:, None, None], moved, state)

    def mine(a):
        return lax.dynamic_slice_in_dim(a, core * half, half, a.ndim - 1)

    swap = [(i, i ^ 1) for i in range(count)]
    swap_pair = [(i, i ^ 2) for i in range(count)]
    up = [(i, i + 4) for i in range(count - 4)]
    down = [(i + 4, i) for i in range(count - 4)]

    other = lax.ppermute(local, "seq", swap)
    core_earlier = jnp.stack([core == 1, core == 0])
    chip = joined(mine(local), mine(other), core_earlier)
    chip_other = lax.ppermute(chip, "seq", swap_pair)
    results = []

    def beside(work, before, arrived):
        arrived, out = lax.optimization_barrier((arrived, work(before)))
        results.append(out)
        return arrived

    chip_other = beside(across_work, chip, chip_other)
    pair_earlier = jnp.stack([across == 1, across == 0])
    group = joined(chip, chip_other, pair_earlier)
    moving = [group[0], group[1]]
    total = [0.0, 0.0]
    factor = [1.0, 1.0]
    for step in range(count // 4 - 1):
        before = moving
        moving = [lax.ppermute(moving[0], "seq", up), lax.ppermute(moving[1], "seq", down)]
        if step < len(line_work):
            moving = beside(line_work[step], before, moving)
        for s in range(2):
            total[s] = total[s] + factor[s] * moving[s][:states].astype(jnp.float32)
            factor[s] = factor[s] * decay(moving[s])
    shape = (states, half)
    total = jnp.stack([jnp.broadcast_to(jnp.asarray(t, jnp.float32), shape) for t in total])
    chip_in = after(total, chip_other, pair_earlier).astype(jnp.bfloat16)
    rest = lax.ppermute(chip_in, "seq", swap)
    low = jnp.where(core == 0, chip_in, rest)
    high = jnp.where(core == 0, rest, chip_in)
    full = jnp.concatenate([low, high], axis=2).astype(jnp.float32)
    for work in line_work[max(count // 4 - 1, 0) :]:
        results.append(work(moving))
    return after(full, other, core_earlier).astype(jnp.bfloat16), results


def per_device(
    hidden, nucleotides, base_embed, x_proj, gate_proj, bc_proj, conv_x, bias_x, conv_bc,
    bias_bc, log_decay, d_skip, out_proj,
):
    taps, inner = conv_x.shape
    length = hidden.shape[1]
    head_count = d_skip.shape[0]
    head_dim = inner // head_count
    states = conv_bc.shape[1] // 2
    width = min(WIDTH, inner)
    blocks = inner // width
    heads = width // head_dim
    chunks = length // CHUNK
    inv_root = states ** (-0.5)

    r = jnp.arange(length)
    rates = log_decay.astype(jnp.float32)
    same = (r[:, None] // CHUNK) == (r[None, :] // CHUNK)
    older = [r[:, None] <= r[None, :], r[:, None] >= r[None, :]]

    def sums(masks):
        return jnp.stack(
            [
                jnp.dot(log_decay[s], masks[s].astype(jnp.bfloat16), preferred_element_type=jnp.float32)
                for s in range(2)
            ]
        )

    cum = sums([same & older[0], same & older[1]])
    left = sums([same & (r[:, None] > r[None, :]), same & (r[:, None] < r[None, :])])
    part = length // 2
    cum_all = sums(older)
    left_all = sums([r[:, None] > r[None, :], r[:, None] < r[None, :]])
    inject = jnp.sqrt(-jnp.expm1(2.0 * rates))
    tail_all = jnp.exp(left_all) * inject
    tail = jnp.exp(left) * inject
    entry = jnp.exp(cum) * inv_root
    row_terms = jnp.log2(inject * inv_root) - cum * LOG2E
    rows_arr = row_terms.reshape(2, blocks, heads, length).transpose(1, 0, 2, 3)
    rows_arr = rows_arr.reshape(blocks, 2 * heads, length)
    cols_arr = jnp.stack([cum * LOG2E, entry, tail], axis=1)
    cols_arr = cols_arr.reshape(2, 3, blocks, heads, length).transpose(2, 4, 0, 1, 3)
    cols_arr = cols_arr.reshape(blocks, length, 6 * heads)
    tail_arr = tail_all.reshape(2, blocks, heads, length).transpose(1, 3, 0, 2)
    tail_arr = tail_arr.reshape(blocks, length, 2 * heads)
    span_logs = jnp.sum(rates.reshape(2, head_count, chunks, CHUNK), axis=3)
    span_logs = jnp.repeat(span_logs.transpose(0, 2, 1), head_dim, axis=2)
    chunk_decay = jnp.exp(span_logs).reshape(2 * chunks, inner)
    shard_decay = jnp.exp(jnp.sum(span_logs, axis=1))
    entry_all = jnp.exp(cum_all) * inv_root
    entry_arr = entry_all.reshape(2, blocks, heads, length).transpose(1, 3, 0, 2)
    entry_arr = entry_arr.reshape(blocks, length, 2 * heads)
    skip = jnp.repeat(d_skip, head_dim)[None]

    inputs = jnp.concatenate(
        [
            strand_inputs(hidden[0], nucleotides, base_embed),
            strand_inputs(hidden[1], 3 - nucleotides, base_embed),
        ],
        axis=0,
    )
    inputs = lax.optimization_barrier(inputs)

    def project(weight):
        out = jnp.dot(inputs, weight, preferred_element_type=jnp.float32)
        return out.astype(jnp.bfloat16).reshape(2, length, -1)

    bc_pre = project(bc_proj)
    x_pre = project(x_proj)
    edge = taps - 1
    low = jnp.concatenate([x_pre[0, -edge:], bc_pre[0, -edge:]], axis=1)
    high = jnp.concatenate([x_pre[1, :edge], bc_pre[1, :edge]], axis=1)
    low, high = neighbours(low, high)
    x_rim = jnp.stack(
        [
            jnp.pad(low[:, :inner], ((8 - edge, 0), (0, 0))),
            jnp.pad(high[:, :inner], ((0, 8 - edge), (0, 0))),
        ]
    )
    bc_ext = [
        jnp.concatenate([low[:, inner:], bc_pre[0]], axis=0),
        jnp.concatenate([bc_pre[1], high[:, inner:]], axis=0),
    ]
    bc_conv = []
    for s in range(2):
        total = bias_bc
        for k in range(taps):
            at = k if s == 0 else edge - k
            total = total + conv_bc[k] * bc_ext[s][at : at + length].astype(jnp.float32)
        bc_conv.append(jax.nn.silu(total).astype(jnp.bfloat16))
    bc_conv = jnp.stack(bc_conv)
    c_rows = bc_conv[..., states:]
    b_cols = bc_conv[..., :states].transpose(0, 2, 1)

    params = pltpu.CompilerParams(dimension_semantics=("arbitrary",), vmem_limit_bytes=48 * 1024 * 1024)
    wide = pl.BlockSpec((2, length, width), lambda i: (0, 0, i))
    state_block = pl.BlockSpec((2, states, width), lambda i: (0, 0, i))
    whole = lambda a: pl.BlockSpec(a.shape, lambda i: (0,) * a.ndim)
    x_conv, local = pl.pallas_call(
        functools.partial(state_kernel, head_dim),
        grid=(blocks,),
        out_shape=(
            jax.ShapeDtypeStruct((2, length, inner), jnp.bfloat16),
            jax.ShapeDtypeStruct((2, states + PAD, inner), jnp.bfloat16),
        ),
        in_specs=[
            wide,
            pl.BlockSpec((2, 8, width), lambda i: (0, 0, i)),
            pl.BlockSpec((taps, width), lambda i: (0, i)),
            pl.BlockSpec((1, width), lambda i: (0, i)),
            pl.BlockSpec((1, length, 2 * heads), lambda i: (i, 0, 0)),
            pl.BlockSpec((2, width), lambda i: (0, i)),
            whole(b_cols),
        ],
        out_specs=(wide, pl.BlockSpec((2, states + PAD, width), lambda i: (0, 0, i))),
        scratch_shapes=[pltpu.VMEM((length + 16, width), jnp.float32)],
        compiler_params=params,
        name="conv_state",
    )(x_pre, x_rim, conv_x, bias_x[None], tail_arr, shard_decay, b_cols)

    def gate_rows(before):
        rows, _ = lax.optimization_barrier((inputs, before))
        out = jnp.dot(rows, gate_proj, preferred_element_type=jnp.float32)
        return out.astype(jnp.bfloat16).reshape(2, length, -1)

    def scan_strand(strand, before):
        x_in, _ = lax.optimization_barrier((x_conv, before))
        return pl.pallas_call(
        functools.partial(scan_kernel, head_dim, strand),
        grid=(blocks,),
        out_shape=jax.ShapeDtypeStruct((length, inner), jnp.bfloat16),
        in_specs=[
            pl.BlockSpec((1, length, width), lambda i: (strand, 0, i)),
            pl.BlockSpec((1, length, 6 * heads), lambda i: (i, 0, 0)),
            pl.BlockSpec((1, 2 * heads, length), lambda i: (i, 0, 0)),
            whole(b_cols),
            whole(c_rows),
            pl.BlockSpec((2 * chunks, width), lambda i: (0, i)),
            pl.BlockSpec((1, width), lambda i: (0, i)),
        ],
        out_specs=pl.BlockSpec((length, width), lambda i: (0, i)),
        scratch_shapes=[pltpu.VMEM((chunks, CHUNK, CHUNK), jnp.float32)],
        compiler_params=params,
        cost_estimate=pl.CostEstimate(
            flops=12 * length * inner * states, bytes_accessed=6 * length * inner, transcendentals=0
        ),
        name="scan",
    )(x_in, cols_arr, rows_arr, b_cols, c_rows, chunk_decay, skip)

    incoming, (z_pre, y_zero, y_one) = entering(
        local,
        states,
        gate_rows,
        [functools.partial(scan_strand, 0), functools.partial(scan_strand, 1)],
    )

    def scan_half(half):
        rows_spec = pl.BlockSpec((2, part, width), lambda i: (0, half, i))
        return pl.pallas_call(
            functools.partial(gate_kernel, head_dim),
            grid=(blocks,),
            out_shape=jax.ShapeDtypeStruct((part, inner), jnp.bfloat16),
            in_specs=[
                pl.BlockSpec((part, width), lambda i: (half, i)),
                pl.BlockSpec((part, width), lambda i: (half, i)),
                rows_spec,
                pl.BlockSpec((1, part, 2 * heads), lambda i: (i, half, 0)),
                pl.BlockSpec((2, part, states), lambda i: (0, half, 0)),
                state_block,
            ],
            out_specs=pl.BlockSpec((part, width), lambda i: (0, i)),
            compiler_params=params,
            cost_estimate=pl.CostEstimate(
                flops=8 * part * inner * states, bytes_accessed=12 * part * inner, transcendentals=0
            ),
            name="gate",
        )(y_zero, y_one, z_pre, entry_arr, c_rows, incoming)

    def out_part(weight, rows):
        return lax.dot_general(
            weight, rows, (((0,), (1,)), ((), ())), preferred_element_type=jnp.float32
        ).astype(jnp.bfloat16)

    if lax.axis_size("chan") == 2:
        size = out_proj.shape[1] // 2
        mine = lax.axis_index("chan")
        send_weight = lax.dynamic_slice_in_dim(out_proj, (1 - mine) * size, size, 1)
        own_weight = lax.dynamic_slice_in_dim(out_proj, mine * size, size, 1)
        first = scan_half(0)
        sent_first = lax.ppermute(out_part(send_weight, first), "chan", [(0, 1), (1, 0)])
        second = scan_half(1)
        sent_second = lax.ppermute(out_part(send_weight, second), "chan", [(0, 1), (1, 0)])
        own = lax.optimization_barrier(out_part(own_weight, jnp.concatenate([first, second])))
        sent = jnp.concatenate([sent_first, sent_second], axis=1)
        return (own.astype(jnp.float32) + sent.astype(jnp.float32)).astype(jnp.bfloat16)
    mixed_in = jnp.concatenate([scan_half(0), scan_half(1)])
    return lax.psum_scatter(
        out_part(out_proj, mixed_in), "chan", scatter_dimension=0, tiled=True
    )


def solution(mesh):
    in_specs = (
        P(None, "seq", None), P("seq"), P(), P(None, "chan"), P(None, "chan"), P(),
        P(None, "chan"), P("chan"), P(), P(), P(None, "chan", "seq"), P("chan"), P("chan", None),
    )
    return jax.shard_map(
        per_device, mesh=mesh, in_specs=in_specs, out_specs=P("chan", "seq"), check_vma=False
    )
```

```python
import functools

import jax
import jax.numpy as jnp
from jax import lax
from jax.experimental import pallas as pl
from jax.experimental.pallas import tpu as pltpu
from jax.sharding import PartitionSpec as P

CHUNK = 128
WIDTH = 256
PAD = 16
LOG2E = 1.4426950408889634


def silu(v):
    return v * (0.5 + 0.5 * jnp.tanh(0.5 * v))


def strand_inputs(hidden_rows, ids, base_embed):
    table = base_embed.astype(jnp.float32)
    pick = ids[:, None]
    low = jnp.where(pick == 0, table[0], table[1])
    high = jnp.where(pick == 2, table[2], table[3])
    looked = jnp.where(pick < 2, low, high)
    return (hidden_rows.astype(jnp.float32) + looked).astype(jnp.bfloat16)


def spread(cols, first, heads, head_dim):
    rows = cols.shape[0]
    per = 128 // head_dim
    lane = lax.broadcasted_iota(jnp.int32, (rows, 128), 1)
    tiles = []
    for t in range(heads // per):
        tile = jnp.broadcast_to(cols[:, first + t * per : first + t * per + 1], (rows, 128))
        for p in range(1, per):
            h = first + t * per + p
            tile = jnp.where(
                lane >= p * head_dim, jnp.broadcast_to(cols[:, h : h + 1], (rows, 128)), tile
            )
        tiles.append(tile)
    return jnp.concatenate(tiles, axis=1)


def state_kernel(head_dim, x_ref, rim_ref, taps_ref, bias_ref, tail_ref, decay_ref, bt_ref, conv_ref, state_ref, ext):
    strands, length, width = x_ref.shape
    taps = taps_ref.shape[0]
    heads = width // head_dim
    for s in range(strands):
        ext[8 : 8 + length] = x_ref[s].astype(jnp.float32)
        if s == 0:
            ext[0:8] = rim_ref[s].astype(jnp.float32)
        else:
            ext[8 + length : 16 + length] = rim_ref[s].astype(jnp.float32)
        chunks = length // CHUNK
        for step in range(chunks):
            c = step if s == 0 else chunks - 1 - step
            total = jnp.broadcast_to(bias_ref[...], (CHUNK, width))
            for k in range(taps):
                shift = k - (taps - 1) if s == 0 else (taps - 1) - k
                start = 8 + c * CHUNK + shift
                total = total + taps_ref[k : k + 1] * ext[start : start + CHUNK]
            rows = slice(c * CHUNK, (c + 1) * CHUNK)
            x = silu(total).astype(jnp.bfloat16)
            conv_ref[s, rows] = x
            scale = spread(tail_ref[0, rows], s * heads, heads, head_dim)
            xs = (x.astype(jnp.float32) * scale).astype(jnp.bfloat16)
            part = jnp.dot(bt_ref[s, :, rows], xs, preferred_element_type=jnp.float32)
            if step == 0:
                acc = part
            else:
                acc = acc + part
        states = acc.shape[0]
        state_ref[s, :states] = acc.astype(state_ref.dtype)
        state_ref[s, states:] = jnp.broadcast_to(
            decay_ref[s : s + 1], (PAD, width)
        ).astype(state_ref.dtype)


def scan_kernel(head_dim, s, x_ref, cols_ref, rows_ref, bt_ref, c_ref, chunk_ref, skip_ref, out_ref, scores):
    _, length, width = x_ref.shape
    heads = width // head_dim
    per = 128 // head_dim
    chunks = length // CHUNK

    @pl.when(pl.program_id(0) == 0)
    def _():
        t = lax.broadcasted_iota(jnp.int32, (CHUNK, CHUNK), 0)
        r = lax.broadcasted_iota(jnp.int32, (CHUNK, CHUNK), 1)
        keep = (r <= t) if s == 0 else (r >= t)
        for c in range(chunks):
            rows = slice(c * CHUNK, (c + 1) * CHUNK)
            sc = jnp.dot(c_ref[s, rows], bt_ref[s, :, rows], preferred_element_type=jnp.float32)
            scores[c] = jnp.where(keep, sc, 0.0)

    lane = lax.broadcasted_iota(jnp.int32, (CHUNK, 128), 1)
    state = None
    order = range(chunks) if s == 0 else range(chunks - 1, -1, -1)
    for step, c in enumerate(order):
        rows = slice(c * CHUNK, (c + 1) * CHUNK)
        cols = cols_ref[0, rows]
        base = s * 3 * heads
        x = x_ref[0, rows]
        sc = scores[c]
        y = skip_ref[...] * x.astype(jnp.float32)
        if step > 0:
            carried = jnp.dot(
                c_ref[s, rows], state.astype(jnp.bfloat16), preferred_element_type=jnp.float32
            )
            y = y + carried * spread(cols, base + heads, heads, head_dim)
        tiles = []
        for t in range(heads // per):
            xt = x[:, t * 128 : (t + 1) * 128]
            lhs, rhs = [], []
            for p in range(per):
                h = t * per + p
                gap = cols[:, base + h : base + h + 1] + rows_ref[0, s * heads + h : s * heads + h + 1, rows]
                lhs.append((sc * jnp.exp2(jnp.minimum(gap, 0.0))).astype(jnp.bfloat16))
                inside = (lane >= p * head_dim) & (lane < (p + 1) * head_dim)
                rhs.append(jnp.where(inside, xt, jnp.zeros_like(xt)))
            tiles.append(
                jnp.dot(
                    jnp.concatenate(lhs, axis=1),
                    jnp.concatenate(rhs, axis=0),
                    preferred_element_type=jnp.float32,
                )
            )
        y = y + jnp.concatenate(tiles, axis=1)
        out_ref[rows] = y.astype(out_ref.dtype)
        if step < chunks - 1:
            scale = spread(cols, base + 2 * heads, heads, head_dim)
            xs = (x.astype(jnp.float32) * scale).astype(jnp.bfloat16)
            fresh = jnp.dot(bt_ref[s, :, rows], xs, preferred_element_type=jnp.float32)
            at = s * chunks + c
            state = fresh if step == 0 else chunk_ref[at : at + 1] * state + fresh


def gate_kernel(head_dim, y_zero, y_one, z_ref, entry_ref, c_ref, in_ref, out_ref):
    strands, length, width = z_ref.shape
    y_refs = (y_zero, y_one)
    heads = width // head_dim
    for c in range(length // CHUNK):
        rows = slice(c * CHUNK, (c + 1) * CHUNK)
        total = 0.0
        for s in range(strands):
            carried = jnp.dot(c_ref[s, rows], in_ref[s], preferred_element_type=jnp.float32)
            y = y_refs[s][rows].astype(jnp.float32)
            y = y + carried * spread(entry_ref[0, rows], s * heads, heads, head_dim)
            total = total + y * silu(z_ref[s, rows].astype(jnp.float32))
        out_ref[rows] = total.astype(out_ref.dtype)


def neighbours(low_rows, high_rows):
    count = lax.axis_size("seq")
    forward = [(i, i + 1) for i in range(count - 1)]
    backward = [(i + 1, i) for i in range(count - 1)]
    return lax.ppermute(low_rows, "seq", forward), lax.ppermute(high_rows, "seq", backward)


def entering(local, states, across_work, line_work):
    count = lax.axis_size("seq")
    me = lax.axis_index("seq")
    half = local.shape[2] // 2
    core, across = me % 2, (me // 2) % 2
    row = lax.broadcasted_iota(jnp.int32, (1, local.shape[1], 1), 1)

    def decay(a):
        return a[..., states : states + 1, :].astype(jnp.float32)

    def joined(first, second, second_is_earlier):
        flag = second_is_earlier[:, None, None]
        a = jnp.where(flag, 1.0, decay(second))
        b = jnp.where(flag, decay(first), 1.0)
        first, second = first.astype(jnp.float32), second.astype(jnp.float32)
        both = jnp.where(row < states, a * first + b * second, first * second)
        return both.astype(jnp.bfloat16)

    def after(state, step, is_earlier):
        moved = decay(step) * state + step[..., :states, :].astype(jnp.float32)
        return jnp.where(is_earlier[:, None, None], moved, state)

    def mine(a):
        return lax.dynamic_slice_in_dim(a, core * half, half, a.ndim - 1)

    swap = [(i, i ^ 1) for i in range(count)]
    swap_pair = [(i, i ^ 2) for i in range(count)]
    up = [(i, i + 4) for i in range(count - 4)]
    down = [(i + 4, i) for i in range(count - 4)]

    other = lax.ppermute(local, "seq", swap)
    core_earlier = jnp.stack([core == 1, core == 0])
    chip = joined(mine(local), mine(other), core_earlier)
    chip_other = lax.ppermute(chip, "seq", swap_pair)
    results = []

    def beside(work, before, arrived):
        arrived, out = lax.optimization_barrier((arrived, work(before)))
        results.append(out)
        return arrived

    chip_other = beside(across_work, chip, chip_other)
    pair_earlier = jnp.stack([across == 1, across == 0])
    group = joined(chip, chip_other, pair_earlier)
    moving = [group[0], group[1]]
    total = [0.0, 0.0]
    factor = [1.0, 1.0]
    for step in range(count // 4 - 1):
        before = moving
        moving = [lax.ppermute(moving[0], "seq", up), lax.ppermute(moving[1], "seq", down)]
        if step < len(line_work):
            moving = beside(line_work[step], before, moving)
        for s in range(2):
            total[s] = total[s] + factor[s] * moving[s][:states].astype(jnp.float32)
            factor[s] = factor[s] * decay(moving[s])
    shape = (states, half)
    total = jnp.stack([jnp.broadcast_to(jnp.asarray(t, jnp.float32), shape) for t in total])
    chip_in = after(total, chip_other, pair_earlier).astype(jnp.bfloat16)
    rest = lax.ppermute(chip_in, "seq", swap)
    low = jnp.where(core == 0, chip_in, rest)
    high = jnp.where(core == 0, rest, chip_in)
    full = jnp.concatenate([low, high], axis=2).astype(jnp.float32)
    for work in line_work[max(count // 4 - 1, 0) :]:
        results.append(work(moving))
    return after(full, other, core_earlier).astype(jnp.bfloat16), results


def per_device(
    hidden, nucleotides, base_embed, x_proj, gate_proj, bc_proj, conv_x, bias_x, conv_bc,
    bias_bc, log_decay, d_skip, out_proj,
):
    taps, inner = conv_x.shape
    length = hidden.shape[1]
    head_count = d_skip.shape[0]
    head_dim = inner // head_count
    states = conv_bc.shape[1] // 2
    width = min(WIDTH, inner)
    blocks = inner // width
    heads = width // head_dim
    chunks = length // CHUNK
    inv_root = states ** (-0.5)

    r = jnp.arange(length)
    rates = log_decay.astype(jnp.float32)
    same = (r[:, None] // CHUNK) == (r[None, :] // CHUNK)
    older = [r[:, None] <= r[None, :], r[:, None] >= r[None, :]]

    def sums(masks):
        return jnp.stack(
            [
                jnp.dot(log_decay[s], masks[s].astype(jnp.bfloat16), preferred_element_type=jnp.float32)
                for s in range(2)
            ]
        )

    cum = sums([same & older[0], same & older[1]])
    left = sums([same & (r[:, None] > r[None, :]), same & (r[:, None] < r[None, :])])
    part = length // 2
    cum_all = sums(older)
    left_all = sums([r[:, None] > r[None, :], r[:, None] < r[None, :]])
    inject = jnp.sqrt(-jnp.expm1(2.0 * rates))
    tail_all = jnp.exp(left_all) * inject
    tail = jnp.exp(left) * inject
    entry = jnp.exp(cum) * inv_root
    row_terms = jnp.log2(inject * inv_root) - cum * LOG2E
    rows_arr = row_terms.reshape(2, blocks, heads, length).transpose(1, 0, 2, 3)
    rows_arr = rows_arr.reshape(blocks, 2 * heads, length)
    cols_arr = jnp.stack([cum * LOG2E, entry, tail], axis=1)
    cols_arr = cols_arr.reshape(2, 3, blocks, heads, length).transpose(2, 4, 0, 1, 3)
    cols_arr = cols_arr.reshape(blocks, length, 6 * heads)
    tail_arr = tail_all.reshape(2, blocks, heads, length).transpose(1, 3, 0, 2)
    tail_arr = tail_arr.reshape(blocks, length, 2 * heads)
    span_logs = jnp.sum(rates.reshape(2, head_count, chunks, CHUNK), axis=3)
    span_logs = jnp.repeat(span_logs.transpose(0, 2, 1), head_dim, axis=2)
    chunk_decay = jnp.exp(span_logs).reshape(2 * chunks, inner)
    shard_decay = jnp.exp(jnp.sum(span_logs, axis=1))
    entry_all = jnp.exp(cum_all) * inv_root
    entry_arr = entry_all.reshape(2, blocks, heads, length).transpose(1, 3, 0, 2)
    entry_arr = entry_arr.reshape(blocks, length, 2 * heads)
    skip = jnp.repeat(d_skip, head_dim)[None]

    inputs = jnp.concatenate(
        [
            strand_inputs(hidden[0], nucleotides, base_embed),
            strand_inputs(hidden[1], 3 - nucleotides, base_embed),
        ],
        axis=0,
    )
    inputs = lax.optimization_barrier(inputs)

    def project(weight):
        out = jnp.dot(inputs, weight, preferred_element_type=jnp.float32)
        return out.astype(jnp.bfloat16).reshape(2, length, -1)

    bc_pre = project(bc_proj)
    x_pre = project(x_proj)
    edge = taps - 1
    low = jnp.concatenate([x_pre[0, -edge:], bc_pre[0, -edge:]], axis=1)
    high = jnp.concatenate([x_pre[1, :edge], bc_pre[1, :edge]], axis=1)
    low, high = neighbours(low, high)
    x_rim = jnp.stack(
        [
            jnp.pad(low[:, :inner], ((8 - edge, 0), (0, 0))),
            jnp.pad(high[:, :inner], ((0, 8 - edge), (0, 0))),
        ]
    )
    bc_ext = [
        jnp.concatenate([low[:, inner:], bc_pre[0]], axis=0),
        jnp.concatenate([bc_pre[1], high[:, inner:]], axis=0),
    ]
    bc_conv = []
    for s in range(2):
        total = bias_bc
        for k in range(taps):
            at = k if s == 0 else edge - k
            total = total + conv_bc[k] * bc_ext[s][at : at + length].astype(jnp.float32)
        bc_conv.append(jax.nn.silu(total).astype(jnp.bfloat16))
    bc_conv = jnp.stack(bc_conv)
    c_rows = bc_conv[..., states:]
    b_cols = bc_conv[..., :states].transpose(0, 2, 1)

    params = pltpu.CompilerParams(dimension_semantics=("arbitrary",), vmem_limit_bytes=48 * 1024 * 1024)
    wide = pl.BlockSpec((2, length, width), lambda i: (0, 0, i))
    state_block = pl.BlockSpec((2, states, width), lambda i: (0, 0, i))
    whole = lambda a: pl.BlockSpec(a.shape, lambda i: (0,) * a.ndim)
    x_conv, local = pl.pallas_call(
        functools.partial(state_kernel, head_dim),
        grid=(blocks,),
        out_shape=(
            jax.ShapeDtypeStruct((2, length, inner), jnp.bfloat16),
            jax.ShapeDtypeStruct((2, states + PAD, inner), jnp.bfloat16),
        ),
        in_specs=[
            wide,
            pl.BlockSpec((2, 8, width), lambda i: (0, 0, i)),
            pl.BlockSpec((taps, width), lambda i: (0, i)),
            pl.BlockSpec((1, width), lambda i: (0, i)),
            pl.BlockSpec((1, length, 2 * heads), lambda i: (i, 0, 0)),
            pl.BlockSpec((2, width), lambda i: (0, i)),
            whole(b_cols),
        ],
        out_specs=(wide, pl.BlockSpec((2, states + PAD, width), lambda i: (0, 0, i))),
        scratch_shapes=[pltpu.VMEM((length + 16, width), jnp.float32)],
        compiler_params=params,
        name="conv_state",
    )(x_pre, x_rim, conv_x, bias_x[None], tail_arr, shard_decay, b_cols)

    def gate_rows(before):
        rows, _ = lax.optimization_barrier((inputs, before))
        out = jnp.dot(rows, gate_proj, preferred_element_type=jnp.float32)
        return out.astype(jnp.bfloat16).reshape(2, length, -1)

    def scan_strand(strand, before):
        x_in, _ = lax.optimization_barrier((x_conv, before))
        return pl.pallas_call(
        functools.partial(scan_kernel, head_dim, strand),
        grid=(blocks,),
        out_shape=jax.ShapeDtypeStruct((length, inner), jnp.bfloat16),
        in_specs=[
            pl.BlockSpec((1, length, width), lambda i: (strand, 0, i)),
            pl.BlockSpec((1, length, 6 * heads), lambda i: (i, 0, 0)),
            pl.BlockSpec((1, 2 * heads, length), lambda i: (i, 0, 0)),
            whole(b_cols),
            whole(c_rows),
            pl.BlockSpec((2 * chunks, width), lambda i: (0, i)),
            pl.BlockSpec((1, width), lambda i: (0, i)),
        ],
        out_specs=pl.BlockSpec((length, width), lambda i: (0, i)),
        scratch_shapes=[pltpu.VMEM((chunks, CHUNK, CHUNK), jnp.float32)],
        compiler_params=params,
        cost_estimate=pl.CostEstimate(
            flops=12 * length * inner * states, bytes_accessed=6 * length * inner, transcendentals=0
        ),
        name="scan",
    )(x_in, cols_arr, rows_arr, b_cols, c_rows, chunk_decay, skip)

    incoming, (z_pre, y_zero, y_one) = entering(
        local,
        states,
        gate_rows,
        [functools.partial(scan_strand, 0), functools.partial(scan_strand, 1)],
    )

    def scan_half(half, before=None):
        entered = incoming
        if before is not None:
            entered, _ = lax.optimization_barrier((incoming, before))
        rows_spec = pl.BlockSpec((2, part, width), lambda i: (0, half, i))
        return pl.pallas_call(
            functools.partial(gate_kernel, head_dim),
            grid=(blocks,),
            out_shape=jax.ShapeDtypeStruct((part, inner), jnp.bfloat16),
            in_specs=[
                pl.BlockSpec((part, width), lambda i: (half, i)),
                pl.BlockSpec((part, width), lambda i: (half, i)),
                rows_spec,
                pl.BlockSpec((1, part, 2 * heads), lambda i: (i, half, 0)),
                pl.BlockSpec((2, part, states), lambda i: (0, half, 0)),
                state_block,
            ],
            out_specs=pl.BlockSpec((part, width), lambda i: (0, i)),
            compiler_params=params,
            cost_estimate=pl.CostEstimate(
                flops=96 * part * inner * states, bytes_accessed=48 * part * inner, transcendentals=0
            ),
            name="gate",
        )(y_zero, y_one, z_pre, entry_arr, c_rows, entered)

    def out_part(weight, rows):
        return lax.dot_general(
            weight, rows, (((0,), (1,)), ((), ())), preferred_element_type=jnp.float32
        ).astype(jnp.bfloat16)

    if lax.axis_size("chan") == 2:
        size = out_proj.shape[1] // 2
        mine = lax.axis_index("chan")
        send_weight = lax.dynamic_slice_in_dim(out_proj, (1 - mine) * size, size, 1)
        own_weight = lax.dynamic_slice_in_dim(out_proj, mine * size, size, 1)
        first = scan_half(0)
        part_first = out_part(send_weight, first)
        sent_first = lax.ppermute(part_first, "chan", [(0, 1), (1, 0)])
        second = scan_half(1, part_first)
        sent_first, second = lax.optimization_barrier((sent_first, second))
        sent_second = lax.ppermute(out_part(send_weight, second), "chan", [(0, 1), (1, 0)])
        own = lax.optimization_barrier(out_part(own_weight, jnp.concatenate([first, second])))
        sent = jnp.concatenate([sent_first, sent_second], axis=1)
        return (own.astype(jnp.float32) + sent.astype(jnp.float32)).astype(jnp.bfloat16)
    mixed_in = jnp.concatenate([scan_half(0), scan_half(1)])
    return lax.psum_scatter(
        out_part(out_proj, mixed_in), "chan", scatter_dimension=0, tiled=True
    )


def solution(mesh):
    in_specs = (
        P(None, "seq", None), P("seq"), P(), P(None, "chan"), P(None, "chan"), P(),
        P(None, "chan"), P("chan"), P(), P(), P(None, "chan", "seq"), P("chan"), P("chan", None),
    )
    return jax.shard_map(
        per_device, mesh=mesh, in_specs=in_specs, out_specs=P("chan", "seq"), check_vma=False
    )
```
